512 devices in a mesh: dp: 64 (over z, y_lo, x), tensor: 8 (over y_hi, core).
Axes of the slice: x: 4, y: 8 (y_hi: 4, y_lo: 2; y = y_hi * 2 + y_lo), z: 8, core: 2. Of those that a mesh axis runs over, the one named last changes fastest.
Arguments:
- tokens: bfloat16 [24576, 16384], P('dp', 'tensor'), may hold values from -6 to 6
- cotangent: bfloat16 [24576, 16384], P('dp', 'tensor'), may hold values from -16 to 16
- left_factor: bfloat16 [192, 16384], P('tensor'), may hold values from -0.125 to 0.125
- right_factor: bfloat16 [192, 16384], P('tensor'), may hold values from -0.125 to 0.125
- panel_rank: int32 [8], replicated, may hold values from 1 to 24, as said below
Outputs:
- token_grad: bfloat16 [24576, 16384], P('dp', 'tensor')
- left_grad: float32 [192, 8, 64, 32], P('tensor', None, 'dp')
- right_grad: float32 [192, 8, 64, 32], P('tensor', None, 'dp')
The draws below stay inside these ranges and needn't reach their ends.
Inputs may be any that keep to these rules, and one draw needn't show every extreme that they name: panel_rank[p] counts the live slots at the start of panel p; at least one panel has all 24 slots live and another has a single live slot.
All inputs are finite; a program needn't handle non-finite values.
Results may differ from the reference program's by a relative error of at most 0.0049.
Values may be sent and summed in bfloat16 or wider, within the bound.
A program may use at most 128 MiB of HBM per device.

```python
import jax
import jax.numpy as jnp

D = 16384
RP = 24
PANELS = 8
RANKS = 192
TOKENS = 24576
FB = 32
N_DP = 64
N_TENSOR = 8


def draw_panel_rank(key, part):
    first_key, second_key, third_key = jax.random.split(jax.random.fold_in(key, 17), 3)
    counts = jax.random.randint(first_key, (PANELS,), 1, RP + 1)
    full_panel = jax.random.randint(second_key, (), 0, PANELS)
    offset = jax.random.randint(third_key, (), 0, PANELS - 1)
    short_panel = (full_panel + 1 + offset) % PANELS
    panel_ids = jnp.arange(PANELS)
    counts = jnp.where(panel_ids == short_panel, 1, counts)
    return jnp.where(panel_ids == full_panel, RP, counts).astype(jnp.int32)


def raised(entries, own_key, source, target, blocks, factor):
    def block_of(dim):
        return (jnp.arange(entries.shape[dim]) // (entries.shape[dim] // blocks)).reshape((-1,) + (1,) * (entries.ndim - 1 - dim))

    first = jax.random.permutation(own_key, blocks)[block_of(target)]
    second = (block_of(target) + blocks // 2) % blocks
    return jnp.where((block_of(source) == first) | (block_of(source) == second), factor * entries, entries)


def level_of(rng, shape, cuts, low, top_value):
    loudness, own = 1.0, jax.random.fold_in(rng, 6)
    for position, shards_of in cuts:
        steps = jnp.exp(jax.random.uniform(jax.random.fold_in(own, position), (shards_of,), jnp.float32, low / len(cuts), top_value / len(cuts)))
        loudness = loudness * jnp.repeat(steps, shape[position] // shards_of).reshape([-1 if axis == position else 1 for axis in range(len(shape))])
    return loudness


def centred(key, extent, spread, bound, cuts=(), held_as=jnp.bfloat16):
    array = jax.random.normal(key, extent, jnp.float32) * spread
    if len(cuts) > 0:
        array = level_of(key, extent, cuts, -0.22, 0.18) * array
    return jnp.clip(array, min=-bound, max=bound).astype(held_as)


def heavy_noise(stream_key, dims, spread, limit, shards, heavy, kind=jnp.bfloat16):
    result = spread * jax.random.normal(stream_key, dims, jnp.float32)
    if shards:
        result = result * level_of(stream_key, dims, shards, -0.22, 0.18)
    return jnp.clip(raised(result, jax.random.fold_in(stream_key, 3), *heavy), -limit, limit).astype(kind)


def setup_inputs(seed: int = 0) -> dict:
    streams_of = jax.random.split(jax.random.key(seed), 6)
    return {
        "tokens": centred(streams_of[0], (TOKENS, D), 1.0, 6.0, ((0, 64), (1, 8))),
        "cotangent": heavy_noise(streams_of[1], (TOKENS, D), 1.0, 16.0, ((0, 64), (1, 8)), (0, 1, 64, 4.0)),
        "left_factor": centred(streams_of[2], (RANKS, D), (D // 8) ** -0.5, 0.125, ((0, 8),)),
        "right_factor": centred(streams_of[3], (RANKS, D), (D // 8) ** -0.5, 0.125, ((0, 8),)),
        "panel_rank": draw_panel_rank(jax.random.fold_in(streams_of[5], 71), 0),
    }


def reference(tokens, cotangent, left_factor, right_factor, panel_rank):
    slots = jnp.arange(RANKS, dtype=jnp.int32)
    limits = jnp.repeat(panel_rank, RP, total_repeat_length=RANKS)
    live_rows = ((slots % RP) < limits).astype(left_factor.dtype)[:, None]
    left_live = left_factor * live_rows
    right_live = right_factor * live_rows
    hidden = jnp.dot(tokens, left_live.T, preferred_element_type=jnp.float32).astype(jnp.bfloat16)
    back_hidden = jnp.dot(cotangent, right_live.T, preferred_element_type=jnp.float32).astype(jnp.bfloat16)
    token_grad = jnp.dot(back_hidden, left_live, preferred_element_type=jnp.float32).astype(jnp.bfloat16)
    grad_scale = TOKENS ** -0.5
    right_grad = jnp.dot(hidden.T, cotangent, preferred_element_type=jnp.float32) * grad_scale
    left_grad = jnp.dot(back_hidden.T, tokens, preferred_element_type=jnp.float32) * grad_scale
    right_grad = right_grad.reshape(RANKS, N_TENSOR, N_DP, FB)
    left_grad = left_grad.reshape(RANKS, N_TENSOR, N_DP, FB)
    return token_grad, left_grad, right_grad
```

```python
import math

import jax
import jax.numpy as jnp
from jax import lax
from jax.sharding import PartitionSpec as P


def local(tokens, cotangent, left_factor, right_factor, panel_rank):
    slot_count = left_factor.shape[0]
    groups = lax.axis_size("tensor")
    width = lax.axis_size("dp")
    all_slots = slot_count * groups
    features = tokens.shape[1]
    block = features // width
    factors = jnp.concatenate((left_factor, right_factor), axis=0)
    cols = lax.all_to_all(factors, "tensor", split_axis=1, concat_axis=0, tiled=True)
    cols = cols.reshape(groups, 2, slot_count, features)
    limits = panel_rank.reshape(groups, 1, 1, 1)
    slots = lax.broadcasted_iota(jnp.int32, (1, 1, slot_count, 1), 2)
    live = cols * (slots < limits).astype(jnp.bfloat16)
    left_live = live[:, 0].reshape(all_slots, features)
    right_live = live[:, 1].reshape(all_slots, features)
    feature_dims = (((1,), (1,)), ((), ()))
    hidden_part = lax.dot_general(
        tokens, left_live, feature_dims, preferred_element_type=jnp.float32
    )
    back_part = lax.dot_general(
        cotangent, right_live, feature_dims, preferred_element_type=jnp.float32
    )
    hidden, back_hidden = lax.psum((hidden_part, back_part), "tensor")
    hidden = hidden.astype(jnp.bfloat16)
    back_hidden = back_hidden.astype(jnp.bfloat16)
    grad_scale = 1.0 / math.sqrt(tokens.shape[0] * width)
    token_dims = (((0,), (0,)), ((), ()))
    left_t = lax.dot_general(tokens, back_hidden, token_dims, preferred_element_type=jnp.float32)
    right_t = lax.dot_general(cotangent, hidden, token_dims, preferred_element_type=jnp.float32)
    both = jnp.concatenate((left_t, right_t), axis=1).astype(jnp.bfloat16)
    both = both.reshape(width, block, 2 * all_slots)
    swapped = lax.all_to_all(both, "dp", split_axis=0, concat_axis=0, tiled=True)
    mine = swapped.astype(jnp.float32).sum(0) * grad_scale
    mine = mine.reshape(block, 2, groups, slot_count).transpose(2, 1, 3, 0)
    home = lax.all_to_all(mine, "tensor", split_axis=0, concat_axis=0, tiled=True)
    home = home.transpose(1, 2, 0, 3)[:, :, :, None, :]
    token_grad = jnp.dot(back_hidden, left_live, preferred_element_type=jnp.float32).astype(
        jnp.bfloat16
    )
    return (token_grad, home[0], home[1])


def solution(mesh):
    placed = (P("dp", "tensor"), P("dp", "tensor"), P("tensor", None), P("tensor", None), P())
    return jax.shard_map(
        local,
        mesh=mesh,
        in_specs=placed,
        out_specs=(P("dp", "tensor"), P("tensor", None, "dp", None), P("tensor", None, "dp", None)),
        check_vma=False,
    )
```

```python
import functools
import math

import jax
import jax.numpy as jnp
from jax import lax
from jax.experimental import pallas as pl
from jax.experimental.pallas import tpu as pltpu
from jax.sharding import PartitionSpec as P

LANES = 128
BF16 = jnp.bfloat16
F32 = jnp.float32


def over_rows(a, b):
    return lax.dot_general(a, b, (((0,), (0,)), ((), ())), preferred_element_type=F32)


def over_lanes(a, b):
    return lax.dot_general(a, b, (((1,), (1,)), ((), ())), preferred_element_type=F32)


def kernel(
    nz, nw, nt, kc, scale,
    rank_ref, facs, tok_hbm, cot_hbm,
    tg_hbm, out_ref,
    tok, cot, raw, pick, spread, rows, hid32, hid16, pair_in, pair, quad_in, hidden,
    part, from_w, from_z, sum_w, sum_z, last_z, last_w, piece, home, tgrad,
    loc, a1s, a1r, aws, awr, azs, azr, b1, b2, b3, b4, cws, cwr, czs, czr, dzs, dzr, dws, dwr, es, er,
):
    d = lax.axis_index("dp")
    t = lax.axis_index("tensor")
    z, w = lax.div(d, nw), lax.rem(d, nw)
    yh, core = lax.div(t, 2), lax.rem(t, 2)
    nh = nt // 2
    k2 = 2 * kc
    tokens, features = tok.shape
    twice = raw.shape[2]
    slots = twice // 2
    half = part.shape[3]
    nq = part.shape[0]
    nwq = sum_w.shape[0]
    split = (3 * k2 // 8) // 16 * 16

    def at_t(k):
        return (d, lax.rem(t + k, nt))

    def at_w(k):
        return (z * nw + lax.rem(w + k, nw), t)

    def at_z(k):
        return (lax.rem(z + k, nz) * nw + w, t)

    def at_h(k):
        return (d, lax.rem(yh + k, nh) * 2 + core)

    mate = (d, t + 1 - 2 * core)

    def send(src, dst, ssem, rsem, dev):
        copy = pltpu.make_async_remote_copy(
            src_ref=src, dst_ref=dst, send_sem=ssem, recv_sem=rsem,
            device_id=dev, device_id_type=pl.DeviceIdType.MESH,
        )
        copy.start()
        return copy

    sent = []
    tiles = (w, nw + w, nw + z)

    def cut(owner, tile):
        return facs.at[:, pl.ds(pl.multiple_of(owner * features + tile * LANES, LANES), LANES)]

    local = [pltpu.make_async_copy(cut(t, tiles[i]), raw.at[i, t], loc.at[i]) for i in range(3)]
    load_cot = pltpu.make_async_copy(cot_hbm, cot, loc.at[3])
    load_tok = pltpu.make_async_copy(tok_hbm, tok, loc.at[4])
    for copy in local:
        copy.start()
    load_cot.start()
    load_tok.start()

    barrier = pltpu.get_barrier_semaphore()
    peers = [at_t(k) for k in range(1, nt)] + [at_w(k) for k in range(1, nw)] + [at_z(k) for k in range(1, nz)]
    for peer in peers:
        pl.semaphore_signal(barrier, inc=1, device_id=peer, device_id_type=pl.DeviceIdType.MESH)
    pl.semaphore_wait(barrier, len(peers))

    first = []
    for i in (2, 0, 1):
        for k in range(1, nt):
            dev = at_t(k)
            first.append(send(cut(dev[1], tiles[i]), raw.at[i, t], a1s.at[k - 1, i], a1r.at[k - 1, i], dev))
    sent += first

    column = lax.broadcasted_iota(jnp.int32, (8, nt * twice), 1)
    slot_c = column
    base_c = jnp.zeros((8, nt * twice), jnp.int32)
    rank_c = jnp.zeros((8, nt * twice), jnp.int32)
    slot_r = lax.broadcasted_iota(jnp.int32, (nt * slots, kc), 0)
    base_r = jnp.zeros((nt * slots, kc), jnp.int32)
    rank_r = jnp.zeros((nt * slots, kc), jnp.int32)
    base = jnp.int32(0)
    for p in range(nt):
        inside = column >= p * twice
        slot_c = jnp.where(inside, column - p * twice, slot_c)
        base_c = jnp.where(inside, base, base_c)
        rank_c = jnp.where(inside, rank_ref[p], rank_c)
        inside = slot_r >= p * slots
        base_r = jnp.where(inside, base - p * slots, base_r)
        rank_r = jnp.where(inside, rank_ref[p] + p * slots, rank_r)
        base = base + rank_ref[p]
    row = lax.broadcasted_iota(jnp.int32, (kc, nt * twice), 0)
    place = jnp.where(slot_c < rank_c, base_c + slot_c, -1)[0:1]
    pick[0:kc, :] = (row == place).astype(F32).astype(BF16)
    slot_c = slot_c - slots
    place = jnp.where((slot_c >= 0) & (slot_c < rank_c), base_c + slot_c, -1)[0:1]
    pick[kc:k2, :] = (row == place).astype(F32).astype(BF16)
    col = lax.broadcasted_iota(jnp.int32, (nt * slots, kc), 1)
    spread[...] = ((col == slot_r + base_r) & (slot_r < rank_r)).astype(F32).astype(BF16)

    for copy in local:
        copy.wait()
    second = []

    def picked(i, low, high):
        return jnp.dot(
            pick[low:high, :], raw[i].reshape(nt * twice, LANES), preferred_element_type=F32
        ).astype(BF16)

    for copy in first[: nt - 1]:
        copy.wait_recv()
    rows[nw + z, split:k2, :] = picked(2, split, k2)
    for k in range(1, nz):
        ref = rows.at[nw + z, split:k2, :]
        second.append(send(ref, ref, azs.at[k - 1], azr.at[k - 1], at_z(k)))
    for copy in first[nt - 1 : 2 * (nt - 1)]:
        copy.wait_recv()
    rows[w, :, :] = picked(0, 0, k2)
    for k in range(1, nw):
        ref = rows.at[w]
        second.append(send(ref, ref, aws.at[k - 1, 0], awr.at[k - 1, 0], at_w(k)))
    for copy in first[2 * (nt - 1) :]:
        copy.wait_recv()
    rows[nw + w, 0:split, :] = picked(1, 0, split)
    for k in range(1, nw):
        ref = rows.at[nw + w, 0:split, :]
        second.append(send(ref, ref, aws.at[k - 1, 1], awr.at[k - 1, 1], at_w(k)))
    sent += second
    load_cot.wait()
    load_tok.wait()
    for copy in second:
        copy.wait_recv()

    left = jnp.concatenate([rows[i, 0:kc, :] for i in range(nw + nz)], axis=1)
    right = jnp.concatenate([rows[i, kc:k2, :] for i in range(nw + nz)], axis=1)
    share = tokens // nt
    hid32[:, :, 0:kc] = over_lanes(tok[...], left).reshape(nt, share, kc)
    hid32[:, :, kc:k2] = over_lanes(cot[...], right).reshape(nt, share, kc)
    hid16[...] = hid32[...].astype(BF16)
    copy = send(hid16.at[pl.ds((1 - core) * nh, nh)], pair_in, b1.at[0], b1.at[1], mate)
    sent.append(copy)
    copy.wait_recv()
    mine = hid32[pl.ds(core * nh, nh)] + pair_in[...].astype(F32)
    pair[...] = mine.astype(BF16)
    swaps = []
    for k in range(1, nh):
        to = lax.rem(yh + k, nh)
        swaps.append(send(pair.at[to], quad_in.at[k - 1], b2.at[0, k - 1], b2.at[1, k - 1], at_h(k)))
    sent += swaps
    total = hid32[core * nh + yh] + pair_in[yh].astype(F32)
    for k in range(1, nh):
        swaps[k - 1].wait_recv()
        total = total + quad_in[k - 1].astype(F32)
    own = core * nh + yh
    hidden[own] = total.astype(BF16)
    shares = []
    for k in range(1, nh):
        ref = hidden.at[own]
        shares.append(send(ref, ref, b3.at[0, k - 1], b3.at[1, k - 1], at_h(k)))
    relay = [send(hidden.at[own], hidden.at[own], b4.at[0, 0], b4.at[1, 0], mate)]
    for k in range(1, nh):
        shares[k - 1].wait_recv()
        ref = hidden.at[core * nh + lax.rem(yh + nh - k, nh)]
        relay.append(send(ref, ref, b4.at[0, k], b4.at[1, k], mate))
    for copy in relay:
        copy.wait_recv()
    sent += shares + relay

    zone = features // nz
    tiles_k = kc // LANES

    def outer(array, columns, slab):
        for zb in range(nz):
            full = over_rows(array[:, zb * zone : (zb + 1) * zone], columns).astype(BF16)
            full = full.reshape(nw, 2, half, kc)
            for j in range(tiles_k):
                for h in range(2):
                    part[slab + 2 * j + h, zb] = full[:, h, :, j * LANES : (j + 1) * LANES]

    back = hidden[:, :, kc:k2].reshape(tokens, kc)
    outer(tok, back, 0)
    third_w, third_z = [], []
    for k in range(1, nw):
        to = lax.rem(w + k, nw)
        third_w.append(
            send(part.at[0 : nq // 2, :, to], from_w.at[k - 1, 0 : nq // 2], cws.at[k - 1, 0], cwr.at[k - 1, 0], at_w(k))
        )
    outer(cot, hidden[:, :, 0:kc].reshape(tokens, kc), nq // 2)
    for k in range(1, nz):
        to = lax.rem(z + k, nz)
        third_z.append(send(part.at[nwq:nq, to], from_z.at[k - 1], czs.at[k - 1], czr.at[k - 1], at_z(k)))
    for k in range(1, nw):
        to = lax.rem(w + k, nw)
        third_w.append(
            send(part.at[nq // 2 : nwq, :, to], from_w.at[k - 1, nq // 2 : nwq], cws.at[k - 1, 1], cwr.at[k - 1, 1], at_w(k))
        )
    sent += third_w + third_z

    for i in range(0, nw + nz, 2):
        both = jnp.concatenate([rows[i, 0:kc, :], rows[i + 1, 0:kc, :]], axis=1)
        tgrad[:, i * LANES : (i + 2) * LANES] = jnp.dot(back, both, preferred_element_type=F32).astype(BF16)
    store_tg = pltpu.make_async_copy(tgrad, tg_hbm, loc.at[5])
    store_tg.start()

    fourth = []
    for copy in third_z:
        copy.wait_recv()
    total = part[nwq:nq, z].astype(F32)
    for k in range(1, nz):
        total = total + from_z[k - 1].astype(F32)
    sum_z[...] = total.astype(BF16)
    for k in range(1, nw):
        to = lax.rem(w + k, nw)
        fourth.append(send(sum_z.at[:, to], last_w.at[k - 1], dws.at[k - 1], dwr.at[k - 1], at_w(k)))
    for copy in third_w:
        copy.wait_recv()
    for q in range(nwq):
        total = part[q, :, w].astype(F32)
        for k in range(1, nw):
            total = total + from_w[k - 1, q].astype(F32)
        sum_w[q] = total.astype(BF16)
    for k in range(1, nz):
        to = lax.rem(z + k, nz)
        fourth.append(send(sum_w.at[:, to], last_z.at[k - 1], dzs.at[k - 1], dzr.at[k - 1], at_z(k)))
    sent += fourth
    for copy in fourth:
        copy.wait_recv()
    sum_a = sum_w[:, z].astype(F32)
    for k in range(1, nz):
        sum_a = sum_a + last_z[k - 1].astype(F32)
    sum_b = sum_z[:, w].astype(F32)
    for k in range(1, nw):
        sum_b = sum_b + last_w[k - 1].astype(F32)
    slabs = [sum_a[q] * scale for q in range(nwq)] + [sum_b[q] * scale for q in range(nq - nwq)]

    def side(first_slab):
        return jnp.concatenate(
            [jnp.concatenate([slabs[first_slab + 2 * j], slabs[first_slab + 2 * j + 1]], axis=0) for j in range(tiles_k)],
            axis=1,
        )

    final = [side(0), side(nq // 2)]
    spare = piece.shape[2] - 4 * half
    if spare:
        final.append(jnp.zeros((spare, kc), F32))
    final = jnp.concatenate(final, axis=0)
    high = final.astype(BF16)
    rest = final - high.astype(F32)
    middle = rest.astype(BF16)
    low = (rest - middle.astype(F32)).astype(BF16)
    chosen = spread[...]
    placed = over_lanes(chosen, high) + over_lanes(chosen, middle) + over_lanes(chosen, low)
    piece[...] = placed.reshape(nt, slots, piece.shape[2])
    fifth = []
    for k in range(1, nt):
        to = lax.rem(t + k, nt)
        fifth.append(send(piece.at[to], home.at[t], es.at[k - 1], er.at[k - 1], at_t(k)))
    home[t] = piece[t]
    for copy in fifth:
        copy.wait_recv()
    out_ref[...] = home[...]
    sent += fifth
    for copy in sent:
        copy.wait_send()
    store_tg.wait()


def fused(sizes, kc, ident, panel_rank, facs, tokens, cotangent):
    nz, nw, nt = sizes
    count, features = tokens.shape
    twice = facs.shape[0]
    slots = twice // 2
    k2 = 2 * kc
    nq = 2 * k2 // LANES
    nwq = 3 * nq // 4
    half = features // (nz * nw * 2)
    wide = max(LANES, 4 * half)
    share = count // nt
    nh = nt // 2
    scale = 1.0 / math.sqrt(count * nz * nw)
    dma = pltpu.SemaphoreType.DMA
    vmem = pltpu.VMEM
    scratch = [
        vmem((count, features), BF16),
        vmem((count, features), BF16),
        vmem((3, nt, twice, LANES), BF16),
        vmem((k2, nt * twice), BF16),
        vmem((nt * slots, kc), BF16),
        vmem((nw + nz, k2, LANES), BF16),
        vmem((nt, share, k2), F32),
        vmem((nt, share, k2), BF16),
        vmem((nh, share, k2), BF16),
        vmem((nh, share, k2), BF16),
        vmem((nh - 1, share, k2), BF16),
        vmem((nt, share, k2), BF16),
        vmem((nq, nz, nw, half, LANES), BF16),
        vmem((nw - 1, nwq, nz, half, LANES), BF16),
        vmem((nz - 1, nq - nwq, nw, half, LANES), BF16),
        vmem((nwq, nz, half, LANES), BF16),
        vmem((nq - nwq, nw, half, LANES), BF16),
        vmem((nz - 1, nwq, half, LANES), BF16),
        vmem((nw - 1, nq - nwq, half, LANES), BF16),
        vmem((nt, slots, wide), F32),
        vmem((nt, slots, wide), F32),
        vmem((count, features), BF16),
        dma((6,)),
        dma((nt - 1, 3)),
        dma((nt - 1, 3)),
        dma((nw - 1, 2)),
        dma((nw - 1, 2)),
        dma((nz - 1,)),
        dma((nz - 1,)),
        dma((2,)),
        dma((2, nh - 1)),
        dma((2, nh - 1)),
        dma((2, nh)),
        dma((nw - 1, 2)),
        dma((nw - 1, 2)),
        dma((nz - 1,)),
        dma((nz - 1,)),
        dma((nz - 1,)),
        dma((nz - 1,)),
        dma((nw - 1,)),
        dma((nw - 1,)),
        dma((nt - 1,)),
        dma((nt - 1,)),
    ]
    anywhere = pl.BlockSpec(memory_space=pl.ANY)
    return pl.pallas_call(
        functools.partial(kernel, nz, nw, nt, kc, scale),
        out_shape=(
            jax.ShapeDtypeStruct((count, features), BF16),
            jax.ShapeDtypeStruct((nt, slots, wide), F32),
        ),
        in_specs=[pl.BlockSpec(memory_space=pltpu.SMEM), anywhere, anywhere, anywhere],
        out_specs=(anywhere, pl.BlockSpec(memory_space=pltpu.VMEM)),
        scratch_shapes=scratch,
        compiler_params=pltpu.CompilerParams(
            collective_id=ident, has_side_effects=True, vmem_limit_bytes=48 << 20
        ),
    )(panel_rank, facs, tokens, cotangent)


def local(sizes, tokens, cotangent, left_factor, right_factor, panel_rank):
    nz, nw, nt = sizes
    facs = jnp.concatenate((left_factor, right_factor), axis=0)
    slots = left_factor.shape[0]
    most = -(-nt * slots // LANES) * LANES
    small = functools.partial(fused, sizes, LANES, 1)
    if most > LANES:
        large = functools.partial(fused, sizes, most, 2)
        grad, home = lax.cond(
            jnp.sum(panel_rank) <= LANES, small, large, panel_rank, facs, tokens, cotangent
        )
    else:
        grad, home = small(panel_rank, facs, tokens, cotangent)
    block = tokens.shape[1] // (nz * nw)
    home = home.transpose(1, 0, 2)[:, :, None, :]
    return (grad, home[..., :block], home[..., block : 2 * block])


def solution(mesh):
    side = math.isqrt(mesh.shape["dp"])
    sizes = (mesh.shape["dp"] // side, side, mesh.shape["tensor"])
    placed = (P("dp", "tensor"), P("dp", "tensor"), P("tensor", None), P("tensor", None), P())
    return jax.shard_map(
        functools.partial(local, sizes),
        mesh=mesh,
        in_specs=placed,
        out_specs=(P("dp", "tensor"), P("tensor", None, "dp", None), P("tensor", None, "dp", None)),
        check_vma=False,
    )
```

```python
import functools
import math

import jax
import jax.numpy as jnp
from jax import lax
from jax.experimental import pallas as pl
from jax.experimental.pallas import tpu as pltpu
from jax.sharding import PartitionSpec as P

LANES = 128
BF16 = jnp.bfloat16
F32 = jnp.float32


def over_rows(a, b):
    return lax.dot_general(a, b, (((0,), (0,)), ((), ())), preferred_element_type=F32)


def over_lanes(a, b):
    return lax.dot_general(a, b, (((1,), (1,)), ((), ())), preferred_element_type=F32)


def kernel(
    nz, nw, nt, kc, scale,
    rank_ref, left_hbm, right_hbm, tok_hbm, cot_hbm,
    tg_hbm, out_ref,
    tok, cot, stage, raw, pick, spread, rows, hid32, hid16, pair_in, pair, quad_in, hidden,
    part_w, part_z, from_w, from_z, sum_w, sum_z, last_z, last_w, piece, home, tgrad,
    loc, ls, a1s, a1r, aws, awr, azs, azr, b1, b2, b3, b4, cws, cwr, czs, czr, dzs, dzr, dws, dwr, es, er,
):
    d = lax.axis_index("dp")
    t = lax.axis_index("tensor")
    z, w = lax.div(d, nw), lax.rem(d, nw)
    yh, core = lax.div(t, 2), lax.rem(t, 2)
    nh, nx = nt // 2, nw // 2
    yl, x = lax.div(w, nx), lax.rem(w, nx)
    k2 = 2 * kc
    tokens, features = tok.shape
    slots = raw.shape[3]
    half = part_w.shape[3]
    nwq = part_w.shape[1]
    nq = nwq + part_z.shape[1]
    split = 3 * kc // 8

    def at_t(k):
        return (d, lax.rem(t + k, nt))

    def at_w(k):
        return (z * nw + lax.rem(w + k, nw), t)

    def at_z(k):
        return (lax.rem(z + k, nz) * nw + w, t)

    def at_h(k):
        return (d, lax.rem(yh + k, nh) * 2 + core)

    mate = (d, t + 1 - 2 * core)

    def describe(src, dst, ssem, rsem, dev):
        return pltpu.make_async_remote_copy(
            src_ref=src, dst_ref=dst, send_sem=ssem, recv_sem=rsem,
            device_id=dev, device_id_type=pl.DeviceIdType.MESH,
        )

    def send(src, dst, ssem, rsem, dev):
        copy = describe(src, dst, ssem, rsem, dev)
        copy.start()
        return copy

    sent = []

    def tiles(column_of):
        return (column_of, nw + column_of, nw + z)

    far = lax.rem(yh + 2, nh)
    ahead, behind = lax.rem(yh + 1, nh), lax.rem(yh + nh - 1, nh)
    near = lax.rem(yh + 2 * yl - 1 + nh, nh)
    targets = [(far, 1 - yl, c, core) for c in range(2)]
    targets += [(near, m, c, 2 + 2 * yl + core) for m in range(2) for c in range(2)]
    targets += [(yh, yl, 1 - core, 6)]
    origins = [2 * far, 2 * far + 1, 2 * ahead, 2 * ahead + 1, 2 * behind, 2 * behind + 1, t + 1 - 2 * core]

    def cut(array, owner, tile):
        return array.at[:, pl.ds(pl.multiple_of(owner * features + tile * LANES, LANES), LANES)]

    sources = (right_hbm, left_hbm)
    local = []
    for side in range(2):
        for i in (2, 0, 1):
            for j, (group, row_of, c, slot) in enumerate(targets):
                tile = tiles(row_of * nx + x)[i]
                local.append(
                    pltpu.make_async_copy(
                        cut(sources[side], group * 2 + c, tile), stage.at[side, i, j], ls.at[side, i, j]
                    )
                )
    for side in range(2):
        for i in range(3):
            local.append(
                pltpu.make_async_copy(cut(sources[side], t, tiles(w)[i]), raw.at[side, i, t], ls.at[side, i, 7])
            )
    load_cot = pltpu.make_async_copy(cot_hbm, cot, loc.at[0])
    load_tok = pltpu.make_async_copy(tok_hbm, tok, loc.at[1])
    for copy in local:
        copy.start()
    load_cot.start()
    load_tok.start()

    barrier = pltpu.get_barrier_semaphore()
    peers = [at_t(k) for k in range(1, nt)]
    peers += [(z * nw + (1 - yl) * nx + x, k) for k in range(nt)]
    peers += [(z * nw + m * nx + lax.rem(x + k, nx), t) for m in range(2) for k in range(1, nx)]
    peers += [at_z(k) for k in range(1, nz)]
    for peer in peers:
        pl.semaphore_signal(barrier, inc=1, device_id=peer, device_id_type=pl.DeviceIdType.MESH)
    pl.semaphore_wait(barrier, len(peers))

    for copy in local:
        copy.wait()
    arrive = [[[], [], []], [[], [], []]]
    for side in range(2):
        for i in (2, 0, 1):
            for j, (group, row_of, c, slot) in enumerate(targets):
                column_of = row_of * nx + x
                dev = (z * nw + column_of, group * 2 + c)
                sent.append(
                    send(stage.at[side, i, j], raw.at[side, i, t], a1s.at[side, j, i], a1r.at[side, slot, i], dev)
                )
                arrive[side][i].append(
                    describe(
                        raw.at[side, i, t], raw.at[side, i, origins[j]], a1s.at[side, j, i], a1r.at[side, j, i], dev
                    )
                )

    slot_c = lax.broadcasted_iota(jnp.int32, (8, nt * slots), 1)
    base_c = jnp.zeros((8, nt * slots), jnp.int32)
    rank_c = jnp.zeros((8, nt * slots), jnp.int32)
    slot_r = lax.broadcasted_iota(jnp.int32, (nt * slots, kc), 0)
    base_r = jnp.zeros((nt * slots, kc), jnp.int32)
    rank_r = jnp.zeros((nt * slots, kc), jnp.int32)
    base = jnp.int32(0)
    for p in range(nt):
        start, stop = base - p * slots, rank_ref[p] + p * slots
        inside = slot_c >= p * slots
        base_c = jnp.where(inside, start, base_c)
        rank_c = jnp.where(inside, stop, rank_c)
        inside = slot_r >= p * slots
        base_r = jnp.where(inside, start, base_r)
        rank_r = jnp.where(inside, stop, rank_r)
        base = base + rank_ref[p]
    row = lax.broadcasted_iota(jnp.int32, (kc, nt * slots), 0)
    place = jnp.where(slot_c < rank_c, base_c + slot_c, -1)[0:1]
    pick[...] = (row == place).astype(F32).astype(BF16)
    col = lax.broadcasted_iota(jnp.int32, (nt * slots, kc), 1)
    spread[...] = ((col == slot_r + base_r) & (slot_r < rank_r)).astype(F32).astype(BF16)

    second = [[], []]

    def picked(side, i, low, high):
        return jnp.dot(
            pick[low:high, :], raw[side, i].reshape(nt * slots, LANES), preferred_element_type=F32
        ).astype(BF16)

    for side in range(2):
        for copy in arrive[side][2]:
            copy.wait_recv()
        rows[side, nw + z, split:kc, :] = picked(side, 2, split, kc)
        for k in range(1, nz):
            ref = rows.at[side, nw + z, split:kc, :]
            second[side].append(send(ref, ref, azs.at[k - 1, side], azr.at[k - 1, side], at_z(k)))
        for copy in arrive[side][0]:
            copy.wait_recv()
        rows[side, w, :, :] = picked(side, 0, 0, kc)
        for k in range(1, nw):
            ref = rows.at[side, w]
            second[side].append(send(ref, ref, aws.at[k - 1, 2 * side], awr.at[k - 1, 2 * side], at_w(k)))
        for copy in arrive[side][1]:
            copy.wait_recv()
        rows[side, nw + w, 0:split, :] = picked(side, 1, 0, split)
        for k in range(1, nw):
            ref = rows.at[side, nw + w, 0:split, :]
            second[side].append(send(ref, ref, aws.at[k - 1, 2 * side + 1], awr.at[k - 1, 2 * side + 1], at_w(k)))
    sent += second[0] + second[1]
    load_cot.wait()
    load_tok.wait()

    share = tokens // nt
    pairs, swaps, shares, relay = [], [[], []], [[], []], []
    arrays = (cot, tok)
    own = core * nh + yh

    def project(side):
        for copy in second[side]:
            copy.wait_recv()
        factor = jnp.concatenate([rows[side, i] for i in range(nw + nz)], axis=1)
        hid32[side] = over_lanes(arrays[side][...], factor).reshape(nt, share, kc)
        hid16[side] = hid32[side, pl.ds((1 - core) * nh, nh)].astype(BF16)
        pairs.append(send(hid16.at[side], pair_in.at[side], b1.at[0, side], b1.at[1, side], mate))

    def pair_up(side):
        pairs[side].wait_recv()
        pair[side] = (hid32[side, pl.ds(core * nh, nh)] + pair_in[side].astype(F32)).astype(BF16)
        for k in range(1, nh):
            to = lax.rem(yh + k, nh)
            swaps[side].append(
                send(pair.at[side, to], quad_in.at[side, k - 1], b2.at[0, side, k - 1], b2.at[1, side, k - 1], at_h(k))
            )

    def settle(side):
        total = hid32[side, own] + pair_in[side, yh].astype(F32)
        for k in range(1, nh):
            swaps[side][k - 1].wait_recv()
            total = total + quad_in[side, k - 1].astype(F32)
        hidden[side, own] = total.astype(BF16)
        for k in range(1, nh):
            ref = hidden.at[side, own]
            shares[side].append(send(ref, ref, b3.at[0, side, k - 1], b3.at[1, side, k - 1], at_h(k)))

    def pass_on(side):
        for copy in shares[side]:
            copy.wait_recv()
        ref = hidden.at[side, pl.ds(core * nh, nh)]
        relay.append(send(ref, ref, b4.at[0, side], b4.at[1, side], mate))

    project(0)
    pair_up(0)
    project(1)
    pair_up(1)
    settle(0)
    settle(1)
    pass_on(0)

    zone = features // nz
    tiles_k = kc // LANES

    def outer(array, columns, slab):
        for zb in range(nz):
            full = over_rows(array[:, zb * zone : (zb + 1) * zone], columns).astype(BF16)
            full = full.reshape(nw, 2, half, kc)
            for j in range(tiles_k):
                for h in range(2):
                    q = slab + 2 * j + h
                    value = full[:, h, :, j * LANES : (j + 1) * LANES]
                    if q < nwq:
                        part_w[:, q, zb] = value
                    else:
                        part_z[zb, q - nwq] = value

    relay[0].wait_recv()
    back = hidden[0].reshape(tokens, kc)
    outer(tok, back, 0)
    third_w, third_z = [], []
    for k in range(1, nw):
        to = lax.rem(w + k, nw)
        third_w.append(
            send(part_w.at[to, 0 : nq // 2], from_w.at[k - 1, 0 : nq // 2], cws.at[k - 1, 0], cwr.at[k - 1, 0], at_w(k))
        )
    pass_on(1)
    for i in range(0, nw + nz, 2):
        both = jnp.concatenate([rows[1, i], rows[1, i + 1]], axis=1)
        tgrad[:, i * LANES : (i + 2) * LANES] = jnp.dot(back, both, preferred_element_type=F32).astype(BF16)
    store_tg = pltpu.make_async_copy(tgrad, tg_hbm, loc.at[2])
    store_tg.start()
    relay[1].wait_recv()
    sent += pairs + swaps[0] + swaps[1] + shares[0] + shares[1] + relay
    outer(cot, hidden[1].reshape(tokens, kc), nq // 2)
    for k in range(1, nz):
        to = lax.rem(z + k, nz)
        third_z.append(send(part_z.at[to], from_z.at[k - 1], czs.at[k - 1], czr.at[k - 1], at_z(k)))
    for k in range(1, nw):
        to = lax.rem(w + k, nw)
        third_w.append(
            send(part_w.at[to, nq // 2 : nwq], from_w.at[k - 1, nq // 2 : nwq], cws.at[k - 1, 1], cwr.at[k - 1, 1], at_w(k))
        )
    sent += third_w + third_z

    fourth = [[], []]
    for side, low, high in ((0, 0, nq // 2), (1, nq // 2, nwq)):
        for copy in third_w[side * (nw - 1) : (side + 1) * (nw - 1)]:
            copy.wait_recv()
        for q in range(low, high):
            total = part_w[w, q].astype(F32)
            for k in range(1, nw):
                total = total + from_w[k - 1, q].astype(F32)
            sum_w[:, q] = total.astype(BF16)
        for k in range(1, nz):
            to = lax.rem(z + k, nz)
            fourth[side].append(
                send(sum_w.at[to, low:high], last_z.at[k - 1, low:high], dzs.at[k - 1, side], dzr.at[k - 1, side], at_z(k))
            )
    for copy in third_z:
        copy.wait_recv()
    total = part_z[z].astype(F32)
    for k in range(1, nz):
        total = total + from_z[k - 1].astype(F32)
    for q in range(nq - nwq):
        sum_z[:, q] = total[q].astype(BF16)
    for k in range(1, nw):
        to = lax.rem(w + k, nw)
        fourth[1].append(send(sum_z.at[to], last_w.at[k - 1], dws.at[k - 1], dwr.at[k - 1], at_w(k)))
    sent += fourth[0] + fourth[1]

    def slab(q):
        if q < nwq:
            total = sum_w[z, q].astype(F32)
            for k in range(1, nz):
                total = total + last_z[k - 1, q].astype(F32)
        else:
            total = sum_z[w, q - nwq].astype(F32)
            for k in range(1, nw):
                total = total + last_w[k - 1, q - nwq].astype(F32)
        return total * scale

    chosen = spread[...]
    fifth = []
    for side in range(2):
        for copy in fourth[side]:
            copy.wait_recv()
        first = side * nq // 2
        final = jnp.concatenate(
            [jnp.concatenate([slab(first + 2 * j), slab(first + 2 * j + 1)], axis=0) for j in range(tiles_k)], axis=1
        )
        spare = piece.shape[3] - 2 * half
        if spare:
            final = jnp.concatenate([final, jnp.zeros((spare, kc), F32)], axis=0)
        high = final.astype(BF16)
        rest = final - high.astype(F32)
        middle = rest.astype(BF16)
        low = (rest - middle.astype(F32)).astype(BF16)
        placed = over_lanes(chosen, high) + over_lanes(chosen, middle) + over_lanes(chosen, low)
        piece[side] = placed.reshape(nt, slots, piece.shape[3])
        for k in range(1, nt):
            to = lax.rem(t + k, nt)
            fifth.append(send(piece.at[side, to], home.at[side, t], es.at[k - 1, side], er.at[k - 1, side], at_t(k)))
        home[side, t] = piece[side, t]
    for copy in fifth:
        copy.wait_recv()
    out_ref[...] = home[...]
    sent += fifth
    for copy in sent:
        copy.wait_send()
    store_tg.wait()


def fused(sizes, kc, ident, panel_rank, left_factor, right_factor, tokens, cotangent):
    nz, nw, nt = sizes
    count, features = tokens.shape
    slots = left_factor.shape[0]
    k2 = 2 * kc
    nq = 2 * k2 // LANES
    nwq = 3 * nq // 4
    half = features // (nz * nw * 2)
    wide = max(LANES, 2 * half)
    share = count // nt
    nh = nt // 2
    scale = 1.0 / math.sqrt(count * nz * nw)
    dma = pltpu.SemaphoreType.DMA
    vmem = pltpu.VMEM
    scratch = [
        vmem((count, features), BF16),
        vmem((count, features), BF16),
        vmem((2, 3, 7, slots, LANES), BF16),
        vmem((2, 3, nt, slots, LANES), BF16),
        vmem((kc, nt * slots), BF16),
        vmem((nt * slots, kc), BF16),
        vmem((2, nw + nz, kc, LANES), BF16),
        vmem((2, nt, share, kc), F32),
        vmem((2, nh, share, kc), BF16),
        vmem((2, nh, share, kc), BF16),
        vmem((2, nh, share, kc), BF16),
        vmem((2, nh - 1, share, kc), BF16),
        vmem((2, nt, share, kc), BF16),
        vmem((nw, nwq, nz, half, LANES), BF16),
        vmem((nz, nq - nwq, nw, half, LANES), BF16),
        vmem((nw - 1, nwq, nz, half, LANES), BF16),
        vmem((nz - 1, nq - nwq, nw, half, LANES), BF16),
        vmem((nz, nwq, half, LANES), BF16),
        vmem((nw, nq - nwq, half, LANES), BF16),
        vmem((nz - 1, nwq, half, LANES), BF16),
        vmem((nw - 1, nq - nwq, half, LANES), BF16),
        vmem((2, nt, slots, wide), F32),
        vmem((2, nt, slots, wide), F32),
        vmem((count, features), BF16),
        dma((3,)),
        dma((2, 3, 8)),
        dma((2, 7, 3)),
        dma((2, 7, 3)),
        dma((nw - 1, 4)),
        dma((nw - 1, 4)),
        dma((nz - 1, 2)),
        dma((nz - 1, 2)),
        dma((2, 2)),
        dma((2, 2, nh - 1)),
        dma((2, 2, nh - 1)),
        dma((2, 2)),
        dma((nw - 1, 2)),
        dma((nw - 1, 2)),
        dma((nz - 1,)),
        dma((nz - 1,)),
        dma((nz - 1, 2)),
        dma((nz - 1, 2)),
        dma((nw - 1,)),
        dma((nw - 1,)),
        dma((nt - 1, 2)),
        dma((nt - 1, 2)),
    ]
    anywhere = pl.BlockSpec(memory_space=pl.ANY)
    return pl.pallas_call(
        functools.partial(kernel, nz, nw, nt, kc, scale),
        out_shape=(
            jax.ShapeDtypeStruct((count, features), BF16),
            jax.ShapeDtypeStruct((2, nt, slots, wide), F32),
        ),
        in_specs=[pl.BlockSpec(memory_space=pltpu.SMEM), anywhere, anywhere, anywhere, anywhere],
        out_specs=(anywhere, pl.BlockSpec(memory_space=pltpu.VMEM)),
        scratch_shapes=scratch,
        compiler_params=pltpu.CompilerParams(
            collective_id=ident, has_side_effects=True, vmem_limit_bytes=48 << 20
        ),
    )(panel_rank, left_factor, right_factor, tokens, cotangent)


def local(sizes, tokens, cotangent, left_factor, right_factor, panel_rank):
    nz, nw, nt = sizes
    slots = left_factor.shape[0]
    most = -(-nt * slots // LANES) * LANES
    small = functools.partial(fused, sizes, LANES, 1)
    if most > LANES:
        large = functools.partial(fused, sizes, most, 2)
        grad, home = lax.cond(
            jnp.sum(panel_rank) <= LANES, small, large, panel_rank, left_factor, right_factor, tokens, cotangent
        )
    else:
        grad, home = small(panel_rank, left_factor, right_factor, tokens, cotangent)
    block = tokens.shape[1] // (nz * nw)
    home = home[..., :block].transpose(0, 2, 1, 3)[:, :, :, None, :]
    return (grad, home[0], home[1])


def solution(mesh):
    side = math.isqrt(mesh.shape["dp"])
    sizes = (mesh.shape["dp"] // side, side, mesh.shape["tensor"])
    placed = (P("dp", "tensor"), P("dp", "tensor"), P("tensor", None), P("tensor", None), P())
    return jax.shard_map(
        functools.partial(local, sizes),
        mesh=mesh,
        in_specs=placed,
        out_specs=(P("dp", "tensor"), P("tensor", None, "dp", None), P("tensor", None, "dp", None)),
        check_vma=False,
    )
```

```python
import functools
import math

import jax
import jax.numpy as jnp
from jax import lax
from jax.experimental import pallas as pl
from jax.experimental.pallas import tpu as pltpu
from jax.sharding import PartitionSpec as P

LANES = 128
BF16 = jnp.bfloat16
F32 = jnp.float32


def over_rows(a, b):
    return lax.dot_general(a, b, (((0,), (0,)), ((), ())), preferred_element_type=F32)


def over_lanes(a, b):
    return lax.dot_general(a, b, (((1,), (1,)), ((), ())), preferred_element_type=F32)


def kernel(
    nz, nw, nt, kc, scale,
    rank_ref, left_hbm, right_hbm, tok_hbm, cot_hbm,
    tg_hbm, out_ref,
    tok, cot, stage_z, stage_w, raw_z, raw_w, pick, spread, rows_w, rows_z, hid32, hid16, shares_in, hidden,
    part_w, part_z, from_w, from_z, sum_w, sum_z, last_z, last_w, piece, home, tgrad,
    loc, ls, a1s, a1r, aws, awr, azs, azr, b2, b3, cws, cwr, czs, czr, dzs, dzr, dws, dwr, es, er,
):
    d = lax.axis_index("dp")
    t = lax.axis_index("tensor")
    z, w = lax.div(d, nw), lax.rem(d, nw)
    yh, core = lax.div(t, 2), lax.rem(t, 2)
    nh, nx = nt // 2, nw // 2
    yl, x = lax.div(w, nx), lax.rem(w, nx)
    k2 = 2 * kc
    tokens, features = tok.shape
    slots = raw_z.shape[2]
    half = part_w.shape[3]
    nwq = part_w.shape[1]
    nq = nwq + part_z.shape[1]
    split = kc // 4

    def at_t(k):
        return (d, lax.rem(t + k, nt))

    def at_w(k):
        return (z * nw + lax.rem(w + k, nw), t)

    def at_z(k):
        return (lax.rem(z + k, nz) * nw + w, t)

    order_z = sorted(range(1, nz), key=lambda k: -min(k, nz - k))
    order_w = sorted(
        range(1, nw), key=lambda k: -(min(k % nx, nx - k % nx) + (k >= nx // 2 and k < nw - nx // 2))
    )
    order_t = sorted(range(1, nt), key=lambda k: -min(k, nt - k))

    def describe(src, dst, ssem, rsem, dev):
        return pltpu.make_async_remote_copy(
            src_ref=src, dst_ref=dst, send_sem=ssem, recv_sem=rsem,
            device_id=dev, device_id_type=pl.DeviceIdType.MESH,
        )

    def send(src, dst, ssem, rsem, dev):
        copy = describe(src, dst, ssem, rsem, dev)
        copy.start()
        return copy

    barrier = pltpu.get_barrier_semaphore()
    peers = [at_t(k) for k in range(1, nt)]
    peers += [(z * nw + (1 - yl) * nx + x, k) for k in range(nt)]
    peers += [(z * nw + m * nx + lax.rem(x + k, nx), t) for m in range(2) for k in range(1, nx)]
    peers += [at_z(k) for k in range(1, nz)]
    for peer in peers:
        pl.semaphore_signal(barrier, inc=1, device_id=peer, device_id_type=pl.DeviceIdType.MESH)

    sent = []

    def tiles(column_of):
        return (column_of, nw + column_of, nw + z)

    far = lax.rem(yh + 2, nh)
    ahead, behind = lax.rem(yh + 1, nh), lax.rem(yh + nh - 1, nh)
    near = lax.rem(yh + 2 * yl - 1 + nh, nh)
    targets = [(far, 1 - yl, c, core) for c in range(2)]
    targets += [(near, m, c, 2 + 2 * yl + core) for m in range(2) for c in range(2)]
    targets += [(yh, yl, 1 - core, 6)]
    origins = [2 * far, 2 * far + 1, 2 * ahead, 2 * ahead + 1, 2 * behind, 2 * behind + 1, t + 1 - 2 * core]

    def cut(array, owner, tile):
        return array.at[:, pl.ds(pl.multiple_of(owner * features + tile * LANES, LANES), LANES)]

    sources = (right_hbm, left_hbm)
    pull = [[[], []], [[], []]]
    keep = [[], []]
    for side in range(2):
        for j, (group, row_of, c, slot) in enumerate(targets):
            tile = tiles(row_of * nx + x)
            owner = group * 2 + c
            pull[side][1].append(
                pltpu.make_async_copy(cut(sources[side], owner, tile[2]), stage_z.at[side, j], ls.at[side, 2, j])
            )
            for i in range(2):
                pull[side][0].append(
                    pltpu.make_async_copy(cut(sources[side], owner, tile[i]), stage_w.at[side, j, i], ls.at[side, i, j])
                )
        mine = tiles(w)
        keep[side].append(pltpu.make_async_copy(cut(sources[side], t, mine[2]), raw_z.at[side, t], ls.at[side, 2, 7]))
        for i in range(2):
            keep[side].append(
                pltpu.make_async_copy(cut(sources[side], t, mine[i]), raw_w.at[side, t, i], ls.at[side, i, 7])
            )
        for copy in pull[side][1] + pull[side][0] + keep[side]:
            copy.start()
    load_cot = pltpu.make_async_copy(cot_hbm, cot, loc.at[0])
    load_tok = pltpu.make_async_copy(tok_hbm, tok, loc.at[1])
    load_cot.start()
    load_tok.start()

    pl.semaphore_wait(barrier, len(peers))

    arrive = [[[], []], [[], []]]
    for side in range(2):
        for kind, stage, raw in ((1, stage_z, raw_z), (0, stage_w, raw_w)):
            for copy in pull[side][kind]:
                copy.wait()
            for j, (group, row_of, c, slot) in enumerate(targets):
                dev = (z * nw + row_of * nx + x, group * 2 + c)
                sems = (a1s.at[side, j, kind], a1r.at[side, slot, kind])
                sent.append(send(stage.at[side, j], raw.at[side, t], sems[0], sems[1], dev))
                arrive[side][kind].append(
                    describe(raw.at[side, t], raw.at[side, origins[j]], sems[0], a1r.at[side, j, kind], dev)
                )

    slot_c = lax.broadcasted_iota(jnp.int32, (8, nt * slots), 1)
    base_c = jnp.zeros((8, nt * slots), jnp.int32)
    rank_c = jnp.zeros((8, nt * slots), jnp.int32)
    slot_r = lax.broadcasted_iota(jnp.int32, (nt * slots, kc), 0)
    base_r = jnp.zeros((nt * slots, kc), jnp.int32)
    rank_r = jnp.zeros((nt * slots, kc), jnp.int32)
    base = jnp.int32(0)
    for p in range(nt):
        start, stop = base - p * slots, rank_ref[p] + p * slots
        inside = slot_c >= p * slots
        base_c = jnp.where(inside, start, base_c)
        rank_c = jnp.where(inside, stop, rank_c)
        inside = slot_r >= p * slots
        base_r = jnp.where(inside, start, base_r)
        rank_r = jnp.where(inside, stop, rank_r)
        base = base + rank_ref[p]
    row = lax.broadcasted_iota(jnp.int32, (kc, nt * slots), 0)
    place = jnp.where(slot_c < rank_c, base_c + slot_c, -1)[0:1]
    pick[...] = (row == place).astype(F32).astype(BF16)
    col = lax.broadcasted_iota(jnp.int32, (nt * slots, kc), 1)
    spread[...] = ((col == slot_r + base_r) & (slot_r < rank_r)).astype(F32).astype(BF16)

    second = [[], []]

    def picked(array, low, high):
        return jnp.dot(
            pick[low:high, :], array.reshape(nt * slots, LANES), preferred_element_type=F32
        ).astype(BF16)

    for side in range(2):
        for copy in keep[side]:
            copy.wait()
        for copy in arrive[side][1]:
            copy.wait_recv()
        rows_z[side, z] = picked(raw_z[side], split, kc)
        for k in order_z:
            ref = rows_z.at[side, z]
            second[side].append(send(ref, ref, azs.at[k - 1, side], azr.at[k - 1, side], at_z(k)))
        for copy in arrive[side][0]:
            copy.wait_recv()
        rows_w[side, w, 0:kc, :] = picked(raw_w[side, :, 0], 0, kc)
        rows_w[side, w, kc : kc + split, :] = picked(raw_w[side, :, 1], 0, split)
        for k in order_w:
            ref = rows_w.at[side, w]
            second[side].append(send(ref, ref, aws.at[k - 1, side], awr.at[k - 1, side], at_w(k)))
    sent += second[0] + second[1]
    load_cot.wait()
    load_tok.wait()

    share = tokens // nt
    swaps, shares = [[], []], [[], []]
    arrays = (cot, tok)

    def block(side, i):
        if i < nw:
            return rows_w[side, i, 0:kc, :]
        return jnp.concatenate([rows_w[side, i - nw, kc : kc + split, :], rows_z[side, i - nw]], axis=0)

    def project(side):
        for copy in second[side]:
            copy.wait_recv()
        factor = jnp.concatenate([block(side, i) for i in range(nw + nz)], axis=1)
        hid32[side] = over_lanes(arrays[side][...], factor).reshape(nt, share, kc)
        hid16[side] = hid32[side].astype(BF16)
        for k in order_t:
            to = lax.rem(t + k, nt)
            swaps[side].append(
                send(hid16.at[side, to], shares_in.at[side, k - 1], b2.at[0, side, k - 1], b2.at[1, side, k - 1], at_t(k))
            )

    def settle(side):
        for copy in swaps[side]:
            copy.wait_recv()
        total = hid32[side, t]
        for k in range(1, nt):
            total = total + shares_in[side, k - 1].astype(F32)
        hidden[side, t] = total.astype(BF16)
        for k in order_t:
            ref = hidden.at[side, t]
            shares[side].append(send(ref, ref, b3.at[0, side, k - 1], b3.at[1, side, k - 1], at_t(k)))

    project(0)
    project(1)
    settle(0)
    settle(1)

    zone = features // nz
    tiles_k = kc // LANES

    def outer(array, columns, slab):
        for zb in range(nz):
            full = over_rows(array[:, zb * zone : (zb + 1) * zone], columns).astype(BF16)
            full = full.reshape(nw, 2, half, kc)
            for j in range(tiles_k):
                for h in range(2):
                    q = slab + 2 * j + h
                    value = full[:, h, :, j * LANES : (j + 1) * LANES]
                    if q < nwq:
                        part_w[:, q, zb] = value
                    else:
                        part_z[zb, q - nwq] = value

    for copy in shares[0]:
        copy.wait_recv()
    back = hidden[0].reshape(tokens, kc)
    outer(tok, back, 0)
    third_w, third_z = [], []
    for k in order_w:
        to = lax.rem(w + k, nw)
        third_w.append(
            send(part_w.at[to, 0 : nq // 2], from_w.at[k - 1, 0 : nq // 2], cws.at[k - 1, 0], cwr.at[k - 1, 0], at_w(k))
        )
    for i in range(0, nw + nz, 2):
        both = jnp.concatenate([block(1, i), block(1, i + 1)], axis=1)
        tgrad[:, i * LANES : (i + 2) * LANES] = jnp.dot(back, both, preferred_element_type=F32).astype(BF16)
    store_tg = pltpu.make_async_copy(tgrad, tg_hbm, loc.at[2])
    store_tg.start()
    for copy in shares[1]:
        copy.wait_recv()
    sent += swaps[0] + swaps[1] + shares[0] + shares[1]
    outer(cot, hidden[1].reshape(tokens, kc), nq // 2)
    for k in order_z:
        to = lax.rem(z + k, nz)
        third_z.append(send(part_z.at[to], from_z.at[k - 1], czs.at[k - 1], czr.at[k - 1], at_z(k)))
    for k in order_w:
        to = lax.rem(w + k, nw)
        third_w.append(
            send(part_w.at[to, nq // 2 : nwq], from_w.at[k - 1, nq // 2 : nwq], cws.at[k - 1, 1], cwr.at[k - 1, 1], at_w(k))
        )
    sent += third_w + third_z

    fourth = [[], []]
    for side, low, high in ((0, 0, nq // 2), (1, nq // 2, nwq)):
        for copy in third_w[side * (nw - 1) : (side + 1) * (nw - 1)]:
            copy.wait_recv()
        for q in range(low, high):
            total = part_w[w, q].astype(F32)
            for k in range(1, nw):
                total = total + from_w[k - 1, q].astype(F32)
            sum_w[:, q] = total.astype(BF16)
        for k in order_z:
            to = lax.rem(z + k, nz)
            fourth[side].append(
                send(sum_w.at[to, low:high], last_z.at[k - 1, low:high], dzs.at[k - 1, side], dzr.at[k - 1, side], at_z(k))
            )
    for copy in third_z:
        copy.wait_recv()
    total = part_z[z].astype(F32)
    for k in order_z:
        total = total + from_z[k - 1].astype(F32)
    for q in range(nq - nwq):
        sum_z[:, q] = total[q].astype(BF16)
    for k in order_w:
        to = lax.rem(w + k, nw)
        fourth[1].append(send(sum_z.at[to], last_w.at[k - 1], dws.at[k - 1], dwr.at[k - 1], at_w(k)))
    sent += fourth[0] + fourth[1]

    def slab(q):
        if q < nwq:
            total = sum_w[z, q].astype(F32)
            for k in range(1, nz):
                total = total + last_z[k - 1, q].astype(F32)
        else:
            total = sum_z[w, q - nwq].astype(F32)
            for k in range(1, nw):
                total = total + last_w[k - 1, q - nwq].astype(F32)
        return total * scale

    chosen = spread[...]
    fifth = []
    for side in range(2):
        for copy in fourth[side]:
            copy.wait_recv()
        first = side * nq // 2
        final = jnp.concatenate(
            [jnp.concatenate([slab(first + 2 * j), slab(first + 2 * j + 1)], axis=0) for j in range(tiles_k)], axis=1
        )
        spare = piece.shape[3] - 2 * half
        if spare:
            final = jnp.concatenate([final, jnp.zeros((spare, kc), F32)], axis=0)
        high = final.astype(BF16)
        rest = final - high.astype(F32)
        middle = rest.astype(BF16)
        low = (rest - middle.astype(F32)).astype(BF16)
        placed = over_lanes(chosen, high) + over_lanes(chosen, middle) + over_lanes(chosen, low)
        piece[side] = placed.reshape(nt, slots, piece.shape[3])
        for k in order_t:
            to = lax.rem(t + k, nt)
            fifth.append(send(piece.at[side, to], home.at[side, t], es.at[k - 1, side], er.at[k - 1, side], at_t(k)))
        home[side, t] = piece[side, t]
    for copy in fifth:
        copy.wait_recv()
    out_ref[...] = home[...]
    sent += fifth
    for copy in sent:
        copy.wait_send()
    store_tg.wait()


def fused(sizes, kc, ident, panel_rank, left_factor, right_factor, tokens, cotangent):
    nz, nw, nt = sizes
    count, features = tokens.shape
    slots = left_factor.shape[0]
    split = kc // 4
    k2 = 2 * kc
    nq = 2 * k2 // LANES
    nwq = 3 * nq // 4
    half = features // (nz * nw * 2)
    wide = max(LANES, 2 * half)
    share = count // nt
    scale = 1.0 / math.sqrt(count * nz * nw)
    dma = pltpu.SemaphoreType.DMA
    vmem = pltpu.VMEM
    scratch = [
        vmem((count, features), BF16),
        vmem((count, features), BF16),
        vmem((2, 7, slots, LANES), BF16),
        vmem((2, 7, 2, slots, LANES), BF16),
        vmem((2, nt, slots, LANES), BF16),
        vmem((2, nt, 2, slots, LANES), BF16),
        vmem((kc, nt * slots), BF16),
        vmem((nt * slots, kc), BF16),
        vmem((2, nw, kc + split, LANES), BF16),
        vmem((2, nz, kc - split, LANES), BF16),
        vmem((2, nt, share, kc), F32),
        vmem((2, nt, share, kc), BF16),
        vmem((2, nt - 1, share, kc), BF16),
        vmem((2, nt, share, kc), BF16),
        vmem((nw, nwq, nz, half, LANES), BF16),
        vmem((nz, nq - nwq, nw, half, LANES), BF16),
        vmem((nw - 1, nwq, nz, half, LANES), BF16),
        vmem((nz - 1, nq - nwq, nw, half, LANES), BF16),
        vmem((nz, nwq, half, LANES), BF16),
        vmem((nw, nq - nwq, half, LANES), BF16),
        vmem((nz - 1, nwq, half, LANES), BF16),
        vmem((nw - 1, nq - nwq, half, LANES), BF16),
        vmem((2, nt, slots, wide), F32),
        vmem((2, nt, slots, wide), F32),
        vmem((count, features), BF16),
        dma((3,)),
        dma((2, 3, 8)),
        dma((2, 7, 2)),
        dma((2, 7, 2)),
        dma((nw - 1, 2)),
        dma((nw - 1, 2)),
        dma((nz - 1, 2)),
        dma((nz - 1, 2)),
        dma((2, 2, nt - 1)),
        dma((2, 2, nt - 1)),
        dma((nw - 1, 2)),
        dma((nw - 1, 2)),
        dma((nz - 1,)),
        dma((nz - 1,)),
        dma((nz - 1, 2)),
        dma((nz - 1, 2)),
        dma((nw - 1,)),
        dma((nw - 1,)),
        dma((nt - 1, 2)),
        dma((nt - 1, 2)),
    ]
    anywhere = pl.BlockSpec(memory_space=pl.ANY)
    return pl.pallas_call(
        functools.partial(kernel, nz, nw, nt, kc, scale),
        out_shape=(
            jax.ShapeDtypeStruct((count, features), BF16),
            jax.ShapeDtypeStruct((2, nt, slots, wide), F32),
        ),
        in_specs=[pl.BlockSpec(memory_space=pltpu.SMEM), anywhere, anywhere, anywhere, anywhere],
        out_specs=(anywhere, pl.BlockSpec(memory_space=pltpu.VMEM)),
        scratch_shapes=scratch,
        compiler_params=pltpu.CompilerParams(
            collective_id=ident, has_side_effects=True, vmem_limit_bytes=48 << 20
        ),
    )(panel_rank, left_factor, right_factor, tokens, cotangent)


def local(sizes, tokens, cotangent, left_factor, right_factor, panel_rank):
    nz, nw, nt = sizes
    slots = left_factor.shape[0]
    most = -(-nt * slots // LANES) * LANES
    small = functools.partial(fused, sizes, LANES, 1)
    if most > LANES:
        large = functools.partial(fused, sizes, most, 2)
        grad, home = lax.cond(
            jnp.sum(panel_rank) <= LANES, small, large, panel_rank, left_factor, right_factor, tokens, cotangent
        )
    else:
        grad, home = small(panel_rank, left_factor, right_factor, tokens, cotangent)
    block = tokens.shape[1] // (nz * nw)
    home = home[..., :block].transpose(0, 2, 1, 3)[:, :, :, None, :]
    return (grad, home[0], home[1])


def solution(mesh):
    side = math.isqrt(mesh.shape["dp"])
    sizes = (mesh.shape["dp"] // side, side, mesh.shape["tensor"])
    placed = (P("dp", "tensor"), P("dp", "tensor"), P("tensor", None), P("tensor", None), P())
    return jax.shard_map(
        functools.partial(local, sizes),
        mesh=mesh,
        in_specs=placed,
        out_specs=(P("dp", "tensor"), P("tensor", None, "dp", None), P("tensor", None, "dp", None)),
        check_vma=False,
    )
```

```python
import functools
import math

import jax
import jax.numpy as jnp
from jax import lax
from jax.experimental import pallas as pl
from jax.experimental.pallas import tpu as pltpu
from jax.sharding import PartitionSpec as P

LANES = 128
BF16 = jnp.bfloat16
F32 = jnp.float32


def over_rows(a, b):
    return lax.dot_general(a, b, (((0,), (0,)), ((), ())), preferred_element_type=F32)


def over_lanes(a, b):
    return lax.dot_general(a, b, (((1,), (1,)), ((), ())), preferred_element_type=F32)


def kernel(
    nz, nw, nt, kc, scale,
    rank_ref, left_hbm, right_hbm, tok_hbm, cot_hbm,
    tg_hbm, out_ref,
    tok, cot, stage_z, stage_w, raw_z, raw_w, pick, spread, rows_w, rows_z, hid32, hid16, shares_in, hidden,
    part_w, part_z, from_w, from_z, sum_w, sum_z, last_z, last_w, piece, home, tgrad,
    loc, ls, a1s, a1r, aws, awr, azs, azr, b2, b3, cws, cwr, czs, czr, dzs, dzr, dws, dwr, es, er,
):
    d = lax.axis_index("dp")
    t = lax.axis_index("tensor")
    z, w = lax.div(d, nw), lax.rem(d, nw)
    yh, core = lax.div(t, 2), lax.rem(t, 2)
    nh, nx = nt // 2, nw // 2
    yl, x = lax.div(w, nx), lax.rem(w, nx)
    k2 = 2 * kc
    tokens, features = tok.shape
    slots = raw_z.shape[2]
    half = part_w.shape[3]
    tiles_k = kc // LANES
    side_w, side_z = 3 * tiles_k, tiles_k
    split = kc // 4

    def at_t(k):
        return (d, lax.rem(t + k, nt))

    def at_w(k):
        return (z * nw + lax.rem(w + k, nw), t)

    def at_z(k):
        return (lax.rem(z + k, nz) * nw + w, t)

    order_z = sorted(range(1, nz), key=lambda k: -min(k, nz - k))
    order_w = sorted(
        range(1, nw), key=lambda k: -(min(k % nx, nx - k % nx) + (k >= nx // 2 and k < nw - nx // 2))
    )
    order_t = sorted(range(1, nt), key=lambda k: -min(k, nt - k))

    def describe(src, dst, ssem, rsem, dev):
        return pltpu.make_async_remote_copy(
            src_ref=src, dst_ref=dst, send_sem=ssem, recv_sem=rsem,
            device_id=dev, device_id_type=pl.DeviceIdType.MESH,
        )

    def send(src, dst, ssem, rsem, dev):
        copy = describe(src, dst, ssem, rsem, dev)
        copy.start()
        return copy

    barrier = pltpu.get_barrier_semaphore()
    peers = [at_t(k) for k in range(1, nt)]
    peers += [(z * nw + (1 - yl) * nx + x, k) for k in range(nt)]
    peers += [(z * nw + m * nx + lax.rem(x + k, nx), t) for m in range(2) for k in range(1, nx)]
    peers += [at_z(k) for k in range(1, nz)]
    for peer in peers:
        pl.semaphore_signal(barrier, inc=1, device_id=peer, device_id_type=pl.DeviceIdType.MESH)

    sent = []

    def tiles(column_of):
        return (column_of, nw + column_of, nw + z)

    far = lax.rem(yh + 2, nh)
    ahead, behind = lax.rem(yh + 1, nh), lax.rem(yh + nh - 1, nh)
    near = lax.rem(yh + 2 * yl - 1 + nh, nh)
    targets = [(far, 1 - yl, c, core) for c in range(2)]
    targets += [(near, m, c, 2 + 2 * yl + core) for m in range(2) for c in range(2)]
    targets += [(yh, yl, 1 - core, 6)]
    origins = [2 * far, 2 * far + 1, 2 * ahead, 2 * ahead + 1, 2 * behind, 2 * behind + 1, t + 1 - 2 * core]

    def cut(array, owner, tile):
        return array.at[:, pl.ds(pl.multiple_of(owner * features + tile * LANES, LANES), LANES)]

    sources = (right_hbm, left_hbm)
    pull = [[[], []], [[], []]]
    keep = [[], []]
    for side in range(2):
        for j, (group, row_of, c, slot) in enumerate(targets):
            tile = tiles(row_of * nx + x)
            owner = group * 2 + c
            pull[side][1].append(
                pltpu.make_async_copy(cut(sources[side], owner, tile[2]), stage_z.at[side, j], ls.at[side, 2, j])
            )
            for i in range(2):
                pull[side][0].append(
                    pltpu.make_async_copy(cut(sources[side], owner, tile[i]), stage_w.at[side, j, i], ls.at[side, i, j])
                )
        mine = tiles(w)
        keep[side].append(pltpu.make_async_copy(cut(sources[side], t, mine[2]), raw_z.at[side, t], ls.at[side, 2, 7]))
        for i in range(2):
            keep[side].append(
                pltpu.make_async_copy(cut(sources[side], t, mine[i]), raw_w.at[side, t, i], ls.at[side, i, 7])
            )
        for copy in pull[side][1] + pull[side][0] + keep[side]:
            copy.start()
    load_cot = pltpu.make_async_copy(cot_hbm, cot, loc.at[0])
    load_tok = pltpu.make_async_copy(tok_hbm, tok, loc.at[1])
    load_cot.start()
    load_tok.start()

    pl.semaphore_wait(barrier, len(peers))

    arrive = [[[], []], [[], []]]
    for side in range(2):
        for kind, stage, raw in ((1, stage_z, raw_z), (0, stage_w, raw_w)):
            for copy in pull[side][kind]:
                copy.wait()
            for j, (group, row_of, c, slot) in enumerate(targets):
                dev = (z * nw + row_of * nx + x, group * 2 + c)
                sems = (a1s.at[side, j, kind], a1r.at[side, slot, kind])
                sent.append(send(stage.at[side, j], raw.at[side, t], sems[0], sems[1], dev))
                arrive[side][kind].append(
                    describe(raw.at[side, t], raw.at[side, origins[j]], sems[0], a1r.at[side, j, kind], dev)
                )

    slot_c = lax.broadcasted_iota(jnp.int32, (8, nt * slots), 1)
    base_c = jnp.zeros((8, nt * slots), jnp.int32)
    rank_c = jnp.zeros((8, nt * slots), jnp.int32)
    slot_r = lax.broadcasted_iota(jnp.int32, (nt * slots, kc), 0)
    base_r = jnp.zeros((nt * slots, kc), jnp.int32)
    rank_r = jnp.zeros((nt * slots, kc), jnp.int32)
    base = jnp.int32(0)
    for p in range(nt):
        start, stop = base - p * slots, rank_ref[p] + p * slots
        inside = slot_c >= p * slots
        base_c = jnp.where(inside, start, base_c)
        rank_c = jnp.where(inside, stop, rank_c)
        inside = slot_r >= p * slots
        base_r = jnp.where(inside, start, base_r)
        rank_r = jnp.where(inside, stop, rank_r)
        base = base + rank_ref[p]
    row = lax.broadcasted_iota(jnp.int32, (kc, nt * slots), 0)
    place = jnp.where(slot_c < rank_c, base_c + slot_c, -1)[0:1]
    pick[...] = (row == place).astype(F32).astype(BF16)
    col = lax.broadcasted_iota(jnp.int32, (nt * slots, kc), 1)
    spread[...] = ((col == slot_r + base_r) & (slot_r < rank_r)).astype(F32).astype(BF16)

    second = [[], []]

    def picked(array, low, high):
        return jnp.dot(
            pick[low:high, :], array.reshape(nt * slots, LANES), preferred_element_type=F32
        ).astype(BF16)

    for side in range(2):
        for copy in keep[side]:
            copy.wait()
        for copy in arrive[side][1]:
            copy.wait_recv()
        rows_z[side, z] = picked(raw_z[side], split, kc)
        for k in order_z:
            ref = rows_z.at[side, z]
            second[side].append(send(ref, ref, azs.at[k - 1, side], azr.at[k - 1, side], at_z(k)))
        for copy in arrive[side][0]:
            copy.wait_recv()
        rows_w[side, w, 0:kc, :] = picked(raw_w[side, :, 0], 0, kc)
        rows_w[side, w, kc : kc + split, :] = picked(raw_w[side, :, 1], 0, split)
        for k in order_w:
            ref = rows_w.at[side, w]
            second[side].append(send(ref, ref, aws.at[k - 1, side], awr.at[k - 1, side], at_w(k)))
    sent += second[0] + second[1]
    load_cot.wait()
    load_tok.wait()

    share = tokens // nt
    swaps, shares = [[], []], [[], []]
    arrays = (cot, tok)

    def block(side, i):
        if i < nw:
            return rows_w[side, i, 0:kc, :]
        return jnp.concatenate([rows_w[side, i - nw, kc : kc + split, :], rows_z[side, i - nw]], axis=0)

    def project(side):
        for copy in second[side]:
            copy.wait_recv()
        factor = jnp.concatenate([block(side, i) for i in range(nw + nz)], axis=1)
        hid32[side] = over_lanes(arrays[side][...], factor).reshape(nt, share, kc)
        hid16[side] = hid32[side].astype(BF16)
        for k in order_t:
            to = lax.rem(t + k, nt)
            swaps[side].append(
                send(hid16.at[side, to], shares_in.at[side, k - 1], b2.at[0, side, k - 1], b2.at[1, side, k - 1], at_t(k))
            )

    def settle(side):
        for copy in swaps[side]:
            copy.wait_recv()
        total = hid32[side, t]
        for k in range(1, nt):
            total = total + shares_in[side, k - 1].astype(F32)
        hidden[side, t] = total.astype(BF16)
        for k in order_t:
            ref = hidden.at[side, t]
            shares[side].append(send(ref, ref, b3.at[0, side, k - 1], b3.at[1, side, k - 1], at_t(k)))

    project(0)
    project(1)
    settle(0)
    settle(1)

    zone = features // nz
    third_w, third_z = [[], []], [[], []]

    def outer(side, array, columns):
        for zb in range(nz):
            full = over_rows(array[:, zb * zone : (zb + 1) * zone], columns).reshape(nw, 4, half, kc)
            for j in range(tiles_k):
                for h in range(4):
                    value = full[:, h, :, j * LANES : (j + 1) * LANES].astype(BF16)
                    if h < 3:
                        part_w[:, side * side_w + 3 * j + h, zb] = value
                    else:
                        part_z[zb, side * side_z + j] = value
        low, high = side * side_w, (side + 1) * side_w
        for k in order_w:
            to = lax.rem(w + k, nw)
            third_w[side].append(
                send(part_w.at[to, low:high], from_w.at[k - 1, low:high], cws.at[k - 1, side], cwr.at[k - 1, side], at_w(k))
            )
        low, high = side * side_z, (side + 1) * side_z
        for k in order_z:
            to = lax.rem(z + k, nz)
            third_z[side].append(
                send(part_z.at[to, low:high], from_z.at[k - 1, low:high], czs.at[k - 1, side], czr.at[k - 1, side], at_z(k))
            )

    for copy in shares[0]:
        copy.wait_recv()
    back = hidden[0].reshape(tokens, kc)
    outer(0, tok, back)
    for i in range(0, nw + nz, 2):
        both = jnp.concatenate([block(1, i), block(1, i + 1)], axis=1)
        tgrad[:, i * LANES : (i + 2) * LANES] = jnp.dot(back, both, preferred_element_type=F32).astype(BF16)
    store_tg = pltpu.make_async_copy(tgrad, tg_hbm, loc.at[2])
    store_tg.start()
    for copy in shares[1]:
        copy.wait_recv()
    sent += swaps[0] + swaps[1] + shares[0] + shares[1]
    outer(1, cot, hidden[1].reshape(tokens, kc))
    sent += third_w[0] + third_z[0] + third_w[1] + third_z[1]

    fourth = [[], []]
    for side in range(2):
        for copy in third_w[side]:
            copy.wait_recv()
        low, high = side * side_w, (side + 1) * side_w
        for q in range(low, high):
            total = part_w[w, q].astype(F32)
            for k in range(1, nw):
                total = total + from_w[k - 1, q].astype(F32)
            sum_w[:, q] = total.astype(BF16)
        for k in order_z:
            to = lax.rem(z + k, nz)
            fourth[side].append(
                send(sum_w.at[to, low:high], last_z.at[k - 1, low:high], dzs.at[k - 1, side], dzr.at[k - 1, side], at_z(k))
            )
        for copy in third_z[side]:
            copy.wait_recv()
        low, high = side * side_z, (side + 1) * side_z
        for q in range(low, high):
            total = part_z[z, q].astype(F32)
            for k in range(1, nz):
                total = total + from_z[k - 1, q].astype(F32)
            sum_z[:, q] = total.astype(BF16)
        for k in order_w:
            to = lax.rem(w + k, nw)
            fourth[side].append(
                send(sum_z.at[to, low:high], last_w.at[k - 1, low:high], dws.at[k - 1, side], dwr.at[k - 1, side], at_w(k))
            )
    sent += fourth[0] + fourth[1]

    def slab(side, j, h):
        if h < 3:
            q = side * side_w + 3 * j + h
            total = sum_w[z, q].astype(F32)
            for k in range(1, nz):
                total = total + last_z[k - 1, q].astype(F32)
        else:
            q = side * side_z + j
            total = sum_z[w, q].astype(F32)
            for k in range(1, nw):
                total = total + last_w[k - 1, q].astype(F32)
        return total * scale

    chosen = spread[...]
    fifth = []
    for side in range(2):
        for copy in fourth[side]:
            copy.wait_recv()
        final = jnp.concatenate(
            [jnp.concatenate([slab(side, j, h) for h in range(4)], axis=0) for j in range(tiles_k)], axis=1
        )
        spare = piece.shape[3] - 4 * half
        if spare:
            final = jnp.concatenate([final, jnp.zeros((spare, kc), F32)], axis=0)
        high = final.astype(BF16)
        rest = final - high.astype(F32)
        middle = rest.astype(BF16)
        low = (rest - middle.astype(F32)).astype(BF16)
        placed = over_lanes(chosen, high) + over_lanes(chosen, middle) + over_lanes(chosen, low)
        piece[side] = placed.reshape(nt, slots, piece.shape[3])
        for k in order_t:
            to = lax.rem(t + k, nt)
            fifth.append(send(piece.at[side, to], home.at[side, t], es.at[k - 1, side], er.at[k - 1, side], at_t(k)))
        home[side, t] = piece[side, t]
    for copy in fifth:
        copy.wait_recv()
    out_ref[...] = home[...]
    sent += fifth
    for copy in sent:
        copy.wait_send()
    store_tg.wait()


def fused(sizes, kc, ident, panel_rank, left_factor, right_factor, tokens, cotangent):
    nz, nw, nt = sizes
    count, features = tokens.shape
    slots = left_factor.shape[0]
    split = kc // 4
    k2 = 2 * kc
    nz_q = k2 // LANES
    nw_q = 3 * nz_q
    half = features // (nz * nw * 4)
    wide = max(LANES, 4 * half)
    share = count // nt
    scale = 1.0 / math.sqrt(count * nz * nw)
    dma = pltpu.SemaphoreType.DMA
    vmem = pltpu.VMEM
    scratch = [
        vmem((count, features), BF16),
        vmem((count, features), BF16),
        vmem((2, 7, slots, LANES), BF16),
        vmem((2, 7, 2, slots, LANES), BF16),
        vmem((2, nt, slots, LANES), BF16),
        vmem((2, nt, 2, slots, LANES), BF16),
        vmem((kc, nt * slots), BF16),
        vmem((nt * slots, kc), BF16),
        vmem((2, nw, kc + split, LANES), BF16),
        vmem((2, nz, kc - split, LANES), BF16),
        vmem((2, nt, share, kc), F32),
        vmem((2, nt, share, kc), BF16),
        vmem((2, nt - 1, share, kc), BF16),
        vmem((2, nt, share, kc), BF16),
        vmem((nw, nw_q, nz, half, LANES), BF16),
        vmem((nz, nz_q, nw, half, LANES), BF16),
        vmem((nw - 1, nw_q, nz, half, LANES), BF16),
        vmem((nz - 1, nz_q, nw, half, LANES), BF16),
        vmem((nz, nw_q, half, LANES), BF16),
        vmem((nw, nz_q, half, LANES), BF16),
        vmem((nz - 1, nw_q, half, LANES), BF16),
        vmem((nw - 1, nz_q, half, LANES), BF16),
        vmem((2, nt, slots, wide), F32),
        vmem((2, nt, slots, wide), F32),
        vmem((count, features), BF16),
        dma((3,)),
        dma((2, 3, 8)),
        dma((2, 7, 2)),
        dma((2, 7, 2)),
        dma((nw - 1, 2)),
        dma((nw - 1, 2)),
        dma((nz - 1, 2)),
        dma((nz - 1, 2)),
        dma((2, 2, nt - 1)),
        dma((2, 2, nt - 1)),
        dma((nw - 1, 2)),
        dma((nw - 1, 2)),
        dma((nz - 1, 2)),
        dma((nz - 1, 2)),
        dma((nz - 1, 2)),
        dma((nz - 1, 2)),
        dma((nw - 1, 2)),
        dma((nw - 1, 2)),
        dma((nt - 1, 2)),
        dma((nt - 1, 2)),
    ]
    anywhere = pl.BlockSpec(memory_space=pl.ANY)
    return pl.pallas_call(
        functools.partial(kernel, nz, nw, nt, kc, scale),
        out_shape=(
            jax.ShapeDtypeStruct((count, features), BF16),
            jax.ShapeDtypeStruct((2, nt, slots, wide), F32),
        ),
        in_specs=[pl.BlockSpec(memory_space=pltpu.SMEM), anywhere, anywhere, anywhere, anywhere],
        out_specs=(anywhere, pl.BlockSpec(memory_space=pltpu.VMEM)),
        scratch_shapes=scratch,
        compiler_params=pltpu.CompilerParams(
            collective_id=ident, has_side_effects=True, vmem_limit_bytes=48 << 20
        ),
    )(panel_rank, left_factor, right_factor, tokens, cotangent)


def local(sizes, tokens, cotangent, left_factor, right_factor, panel_rank):
    nz, nw, nt = sizes
    slots = left_factor.shape[0]
    most = -(-nt * slots // LANES) * LANES
    small = functools.partial(fused, sizes, LANES, 1)
    if most > LANES:
        large = functools.partial(fused, sizes, most, 2)
        grad, home = lax.cond(
            jnp.sum(panel_rank) <= LANES, small, large, panel_rank, left_factor, right_factor, tokens, cotangent
        )
    else:
        grad, home = small(panel_rank, left_factor, right_factor, tokens, cotangent)
    block = tokens.shape[1] // (nz * nw)
    home = home[..., :block].transpose(0, 2, 1, 3)[:, :, :, None, :]
    return (grad, home[0], home[1])


def solution(mesh):
    side = math.isqrt(mesh.shape["dp"])
    sizes = (mesh.shape["dp"] // side, side, mesh.shape["tensor"])
    placed = (P("dp", "tensor"), P("dp", "tensor"), P("tensor", None), P("tensor", None), P())
    return jax.shard_map(
        functools.partial(local, sizes),
        mesh=mesh,
        in_specs=placed,
        out_specs=(P("dp", "tensor"), P("tensor", None, "dp", None), P("tensor", None, "dp", None)),
        check_vma=False,
    )
```
